32 devices in a mesh: branch: 2 (over core), dap: 4 (over z), rep: 4 (over y, x).
Axes of the slice: x: 2, y: 2, z: 4, core: 2. Of those that a mesh axis runs over, the one named last changes fastest.
Arguments:
- homolog_stack: bfloat16 [512, 32, 256], P(('rep', 'branch', 'dap')), parts along dimension 0, may hold values from -6 to 6
- homolog_validity_flags: int32 [512], P(('rep', 'branch', 'dap')), parts along dimension 0, may hold values 0 or 1
- amino_validity_flags: int32 [128], P('rep'), parts along dimension 0, may hold values from 0 to 1, as said below
- offset_classes: int32 [128, 32], P(('rep', 'branch', 'dap')), parts along dimension 0, may hold values from 0 to 65
- couple_matrix: bfloat16 [128, 32, 128], P(('rep', 'branch', 'dap')), parts along dimension 0, may hold values from -6 to 6
- homolog_standardizer_factor: float32 [256], replicated, may hold values from 0.25 to 1.75
- first_factor_projector: bfloat16 [256, 32], replicated, may hold values from -0.375 to 0.375
- second_factor_projector: bfloat16 [256, 32], replicated, may hold values from -0.375 to 0.375
- product_final_projector: bfloat16 [1024, 128], replicated, may hold values from -0.1875 to 0.1875
- offset_embedding_matrix: bfloat16 [66, 128], replicated, may hold values from -6 to 6
- couple_standardizer_factor: float32 [128], replicated, may hold values from 0.25 to 1.75
- trilateral_edge_projectors: bfloat16 [128, 512], replicated, may hold values from -0.5 to 0.5
- trilateral_sigmoid_projector: bfloat16 [128, 128], replicated, may hold values from -0.5 to 0.5
- trilateral_final_projector: bfloat16 [128, 128], replicated, may hold values from -0.5 to 0.5
- trilateral_standardizer_factor: float32 [128], replicated, may hold values from 0.25 to 1.75
Outputs:
- pair_out: bfloat16 [128, 32, 128], P(('rep', 'branch', 'dap')), parts along dimension 0
The draws below stay inside these ranges and needn't reach their ends.
There are 4 independent parts, one for each index of `rep`. The reference program is written for one: setup_inputs(seed, part) draws one part's arguments, and reference() takes and returns one part's arrays. A program takes and returns all parts, laid end to end along the dimension named above; an argument that names none is the same for every part. Nothing has to cross between parts.
Inputs may be any that keep to these rules, and one draw needn't show every extreme that they name: `amino_validity_flags`: 0 or 1; exactly 12 residues are 0, at any positions.
All inputs are finite; a program needn't handle non-finite values. No bound on the sum of `homolog_validity_flags` on one device may be relied on, other than what follows from the above.
Results may differ from the reference program's by a relative error of at most 0.0036.
Values may be sent and summed in bfloat16 or wider, within the bound.
A program may use at most 64 MiB of HBM per device.

```python
import jax
import jax.numpy as jnp
from jax import lax

FEATURE_DEPTH = 256
CZ = 128
PRODUCT_DEPTH = 32
NBINS = 66
HOMOLOG_TOTAL = 128
AMINO_TOTAL = 32


def draw_amino_validity_flags(key, part):
    order = jax.random.permutation(jax.random.fold_in(key, 7103), AMINO_TOTAL)
    padded = 3 * AMINO_TOTAL // 8
    return (order >= padded).astype(jnp.int32)


def plant(array, stream_key, least, largest):
    extent = array.shape
    spot = [jax.random.randint(jax.random.fold_in(stream_key, axis), (), 0, extent[axis]) for axis in range(len(extent))]
    array = array.at[tuple(spot)].set(least)
    longest = extent.index(max(extent))
    spot[longest] = (spot[longest] + 1) % extent[longest]
    return array.at[tuple(spot)].set(largest)


def levels(stream_key, extent, split, smallest, largest):
    def one(dim, shards_of):
        steps = jax.random.uniform(jax.random.fold_in(jax.random.fold_in(stream_key, 6), dim), (shards_of,), jnp.float32, smallest / len(split), largest / len(split))
        return jnp.repeat(jnp.exp(steps), extent[dim] // shards_of).reshape((-1,) + (1,) * (len(extent) - dim - 1))

    level = one(*split[0])
    for cut in split[1:]:
        level = level * one(*cut)
    return level


def bell_draw(rng, extent, deviation, most, shards=(), held_as=jnp.bfloat16):
    result = deviation * jax.random.normal(rng, extent, jnp.float32)
    if shards:
        result = result * levels(rng, extent, shards, -0.22, 0.18)
    return jnp.clip(result, -most, most).astype(held_as)


def setup_inputs(seed: int = 0, part: int = 0) -> dict:
    keys = jax.random.split(jax.random.key(seed), 16)
    own_keys = jax.random.split(jax.random.fold_in(keys[15], part), 16)
    homolog_stack = bell_draw(own_keys[0], (HOMOLOG_TOTAL, AMINO_TOTAL, FEATURE_DEPTH), 1.0, 6.0, ((0, 8),))
    homolog_validity_flags = plant((jax.random.randint(own_keys[1], (HOMOLOG_TOTAL,), 0, 4) < 3).astype(jnp.int32), jax.random.fold_in(own_keys[1], 1), 0, 1)
    amino_validity_flags = draw_amino_validity_flags(jax.random.fold_in(jax.random.fold_in(keys[15], part), 71), part)
    offset_classes = plant(jax.random.randint(own_keys[3], (AMINO_TOTAL, AMINO_TOTAL), 0, NBINS), jax.random.fold_in(own_keys[3], 1), 0, NBINS - 1).astype(jnp.int32)
    couple_matrix = bell_draw(own_keys[4], (AMINO_TOTAL, AMINO_TOTAL, CZ), 1.0, 6.0, ((0, 8),))
    homolog_standardizer_factor = jnp.clip(1.0 + 0.15 * jax.random.normal(keys[5], (FEATURE_DEPTH,), jnp.float32), 0.25, 1.75)
    first_factor_projector = bell_draw(keys[6], (FEATURE_DEPTH, PRODUCT_DEPTH), FEATURE_DEPTH ** -0.5, 0.375)
    second_factor_projector = bell_draw(keys[7], (FEATURE_DEPTH, PRODUCT_DEPTH), FEATURE_DEPTH ** -0.5, 0.375)
    product_final_projector = bell_draw(keys[8], (PRODUCT_DEPTH * PRODUCT_DEPTH, CZ), (PRODUCT_DEPTH * PRODUCT_DEPTH) ** -0.5, 0.1875)
    offset_embedding_matrix = bell_draw(keys[9], (NBINS, CZ), 1.0, 6.0)
    couple_standardizer_factor = jnp.clip(1.0 + 0.15 * jax.random.normal(keys[10], (CZ,), jnp.float32), 0.25, 1.75)
    trilateral_edge_projectors = bell_draw(keys[11], (CZ, 4 * CZ), CZ ** -0.5, 0.5)
    trilateral_sigmoid_projector = bell_draw(keys[12], (CZ, CZ), CZ ** -0.5, 0.5)
    trilateral_final_projector = bell_draw(keys[13], (CZ, CZ), CZ ** -0.5, 0.5)
    trilateral_standardizer_factor = jnp.clip(1.0 + 0.15 * jax.random.normal(keys[14], (CZ,), jnp.float32), 0.25, 1.75)
    return dict(homolog_stack=homolog_stack, homolog_validity_flags=homolog_validity_flags, amino_validity_flags=amino_validity_flags, offset_classes=offset_classes, couple_matrix=couple_matrix, homolog_standardizer_factor=homolog_standardizer_factor, first_factor_projector=first_factor_projector, second_factor_projector=second_factor_projector, product_final_projector=product_final_projector, offset_embedding_matrix=offset_embedding_matrix, couple_standardizer_factor=couple_standardizer_factor, trilateral_edge_projectors=trilateral_edge_projectors, trilateral_sigmoid_projector=trilateral_sigmoid_projector, trilateral_final_projector=trilateral_final_projector, trilateral_standardizer_factor=trilateral_standardizer_factor)


def standardize_features(values, gain):
    mean = lax.optimization_barrier(jnp.mean(values, axis=-1, keepdims=True))
    centred = values - mean
    spread = lax.optimization_barrier(jnp.mean(centred * centred, axis=-1, keepdims=True))
    return centred * lax.rsqrt(spread + 1e-05) * gain

def reference(homolog_stack, homolog_validity_flags, amino_validity_flags, offset_classes, couple_matrix, homolog_standardizer_factor, first_factor_projector, second_factor_projector, product_final_projector, offset_embedding_matrix, couple_standardizer_factor, trilateral_edge_projectors, trilateral_sigmoid_projector, trilateral_final_projector, trilateral_standardizer_factor):
    plain_real_kind = jnp.float32
    standardized_source = standardize_features(homolog_stack.astype(plain_real_kind), homolog_standardizer_factor).astype(jnp.bfloat16)
    res_all = amino_validity_flags.astype(plain_real_kind)
    rows_live = homolog_validity_flags.astype(plain_real_kind)
    live = rows_live[:, None] * res_all[None, :]
    left = (jnp.einsum('src,cd->srd', standardized_source.astype(plain_real_kind), first_factor_projector.astype(plain_real_kind)) * live[:, :, None]).astype(jnp.bfloat16)
    right = (jnp.einsum('src,cd->srd', standardized_source.astype(plain_real_kind), second_factor_projector.astype(plain_real_kind)) * live[:, :, None]).astype(jnp.bfloat16)
    outer = jnp.einsum('sic,sje->ijce', left.astype(plain_real_kind), right.astype(plain_real_kind))
    amino_total = couple_matrix.shape[0]
    width = couple_matrix.shape[2]
    inner = first_factor_projector.shape[1]
    projected = jnp.dot(outer.reshape(amino_total * amino_total, inner * inner), product_final_projector.astype(plain_real_kind), precision=lax.Precision.HIGHEST).reshape(amino_total, amino_total, width)
    pair_live = res_all[:, None] * res_all[None, :]
    count = jnp.maximum(jnp.sum(rows_live) * pair_live, 1.0)
    onehot = (offset_classes[..., None] == jnp.arange(offset_embedding_matrix.shape[0], dtype=jnp.int32)).astype(plain_real_kind)
    embed = jnp.einsum('ijb,bc->ijc', onehot, offset_embedding_matrix.astype(plain_real_kind))
    updated = couple_matrix.astype(plain_real_kind) + embed + projected / count[..., None]
    normed_pair = standardize_features(updated, couple_standardizer_factor).astype(jnp.bfloat16)
    four = jnp.einsum('ijc,cd->ijd', normed_pair.astype(plain_real_kind), trilateral_edge_projectors.astype(plain_real_kind))
    tri_left = (jax.nn.sigmoid(four[..., :width]) * four[..., width:2 * width] * pair_live[..., None]).astype(jnp.bfloat16)
    tri_right = (jax.nn.sigmoid(four[..., 2 * width:3 * width]) * four[..., 3 * width:] * pair_live[..., None]).astype(jnp.bfloat16)
    triangle = jnp.einsum('ikc,jkc->ijc', tri_left.astype(plain_real_kind), tri_right.astype(plain_real_kind))
    triangle_normed = standardize_features(triangle, trilateral_standardizer_factor).astype(jnp.bfloat16)
    gate = jax.nn.sigmoid(jnp.einsum('ijc,cd->ijd', normed_pair.astype(plain_real_kind), trilateral_sigmoid_projector.astype(plain_real_kind)))
    change = jnp.einsum('ijc,cd->ijd', triangle_normed.astype(plain_real_kind), trilateral_final_projector.astype(plain_real_kind))
    return (updated + gate * change).astype(jnp.bfloat16)
```

```python
import functools

import jax
import jax.numpy as jnp
from jax import lax
from jax.experimental import pallas as pl
from jax.experimental.pallas import tpu as pltpu
from jax.sharding import PartitionSpec as P

F32 = jnp.float32
BF16 = jnp.bfloat16
MESH = pl.DeviceIdType.MESH
LANES = 128
SUB = 8


def iota(shape, axis):
    return lax.broadcasted_iota(jnp.int32, shape, axis)


def dot(a, b):
    return jnp.dot(a, b, preferred_element_type=F32)


def standardize(values, gain):
    mean = jnp.mean(values, axis=-1, keepdims=True)
    centred = values - mean
    spread = jnp.mean(centred * centred, axis=-1, keepdims=True)
    return centred * lax.rsqrt(spread + 1e-05) * gain


def kernel(
    nb, nz,
    x_ref, hflag_ref, aflag_ref, class_ref, couple_ref, hgain_ref, wl_ref, wr_ref, wout_ref,
    embed_ref, cgain_ref, wedge_ref, wgate_ref, wfin_ref, tgain_ref,
    out_ref,
    flag_all, right_all, left_send, left_all, tri_all, y_left, outer_buf, w_wide, w_perm, tri_buf,
    flag_ssem, flag_rsem, right_ssem, right_rsem, right_fsem, left_ssem, left_rsem,
    tri_ssem, tri_rsem, tri_fsem,
):
    n = nb * nz
    branch = lax.axis_index("branch")
    dap = lax.axis_index("dap")
    me = branch * nz + dap
    amino = aflag_ref.shape[1]
    seqs = hflag_ref.shape[1]
    rows = class_ref.shape[0]
    inner = wl_ref.shape[1]
    width = couple_ref.shape[1]
    reps = LANES // inner
    live = amino - 3 * amino // 8
    groups = live // reps
    pairs = rows * amino
    padded = -(-live // SUB) * SUB
    first = me * rows

    same = [(branch, lax.rem(dap + step, nz)) for step in range(1, nz)]
    here = [(lax.rem(branch + step, nb), dap) for step in range(1, nb)]
    far = [(b[0], z[1]) for b in here for z in same]
    near = same + here
    everyone = near + far

    def index_of(peer):
        return peer[0] * nz + peer[1]

    def target(peer):
        return {"branch": peer[0], "dap": peer[1]}

    barrier = pltpu.get_barrier_semaphore()
    for peer in everyone:
        pl.semaphore_signal(barrier, inc=1, device_id=target(peer), device_id_type=MESH)

    aflag = jnp.broadcast_to(aflag_ref[...].astype(F32), (SUB, amino)).astype(BF16)
    hflag32 = hflag_ref[...].astype(F32)
    hflag = jnp.broadcast_to(hflag32, (SUB, seqs)).astype(BF16)

    def lane_keys(lanes):
        r = iota((amino, lanes), 0)
        k = lax.rem(iota((amino, lanes), 1), amino)
        count = dot(aflag, (r <= k).astype(BF16))
        alive = dot(aflag, (r == k).astype(BF16))
        return (count * alive)[0:1, :]

    flag_all[me] = jnp.broadcast_to(jnp.sum(hflag32, axis=1, keepdims=True), (SUB, LANES))

    total = seqs * amino
    key_x = lane_keys(total)
    hlane = dot(hflag, (iota((seqs, total), 0) == iota((seqs, total), 1) // amino).astype(BF16))[0:1, :]
    key_x = jnp.where(hlane > 0.5, key_x, 0.0).astype(jnp.int32)
    m_row = iota((live * seqs, 1), 0)
    same_seq = lax.rem(m_row, seqs) == iota((1, total), 1) // amino
    gather_right = jnp.where((key_x == m_row // seqs + 1) & same_seq, 1.0, 0.0).astype(BF16)
    lane_group = iota((1, LANES), 1) // inner
    alane = dot(
        aflag,
        (iota((amino, amino * inner), 0) == iota((amino, amino * inner), 1) // inner).astype(BF16),
    )[0:1, :]

    normed = standardize(x_ref[...].astype(F32), hgain_ref[...]).astype(BF16)
    w_both = jnp.concatenate([wl_ref[...]] * reps + [wr_ref[...]] * reps, axis=1)
    sides = dot(normed, w_both)
    y_left[...] = sides[:, :LANES]
    right_rows = dot(gather_right, sides[:, LANES:].astype(BF16))
    for q in range(groups):
        block = right_rows[q * reps * seqs : (q * reps + 1) * seqs]
        for g in range(1, reps):
            start = (q * reps + g) * seqs
            block = jnp.where(lane_group == g, right_rows[start : start + seqs], block)
        right_all[me, :, q * LANES : (q + 1) * LANES] = block.astype(BF16)
    for d in range(n):
        block = y_left[pl.ds(d * rows, seqs, stride=amino), :]
        for g in range(1, rows):
            block = jnp.where(
                lane_group == g, y_left[pl.ds(d * rows + g, seqs, stride=amino), :], block
            )
        left_send[d] = (block * alane[:, d * LANES : (d + 1) * LANES]).astype(BF16)

    pl.semaphore_wait(barrier, n - 1)

    sends = []

    def push(src, dst, ssem, rsem, peer):
        copy = pltpu.make_async_remote_copy(
            src_ref=src, dst_ref=dst, send_sem=ssem, recv_sem=rsem,
            device_id=target(peer), device_id_type=MESH,
        )
        copy.start()
        sends.append(copy)

    def arrived(ref, slot, rsem):
        pltpu.make_async_remote_copy(
            src_ref=ref.at[slot], dst_ref=ref.at[slot], send_sem=rsem.at[slot],
            recv_sem=rsem.at[slot], device_id=target(everyone[0]), device_id_type=MESH,
        ).wait_recv()

    for peer in near:
        push(right_all.at[me], right_all.at[me], right_ssem.at[index_of(peer)], right_rsem.at[me], peer)
    for peer in everyone:
        d = index_of(peer)
        push(left_send.at[d], left_all.at[me], left_ssem.at[d], left_rsem.at[me], peer)
        push(flag_all.at[me], flag_all.at[me], flag_ssem.at[d], flag_rsem.at[me], peer)
    left_all[me] = left_send[me]

    w_wide[...] = wout_ref[...].astype(F32)
    for e in range(inner):
        w_perm[e * inner : (e + 1) * inner, :] = w_wide[
            pl.ds(e, inner, stride=inner), :
        ].astype(BF16)
    eye = iota((amino, amino), 0) == iota((amino, amino), 1)
    bins = embed_ref.shape[0]
    hot = []
    for i in range(rows):
        column = jnp.sum(
            jnp.where(eye, class_ref[i : i + 1, :], 0).astype(F32), axis=1, keepdims=True
        ).astype(jnp.int32)
        hot.append(jnp.where(column == iota((amino, bins), 1), 1.0, 0.0))
    onehot = jnp.concatenate(hot, axis=0).astype(BF16)
    base = couple_ref[...].astype(F32) + dot(onehot, embed_ref[...])

    key_pair = lane_keys(pairs)
    ilane = dot(
        aflag, (iota((amino, pairs), 0) == first + iota((amino, pairs), 1) // amino).astype(BF16)
    )[0:1, :]
    key_pair = jnp.where(ilane > 0.5, key_pair, 0.0).astype(jnp.int32)
    pair_row = iota((1, pairs), 1) // amino
    sel_rows = live * rows
    sel_m = iota((sel_rows, 1), 0)
    sel_key = key_pair == sel_m // rows + 1
    select_right = jnp.where(sel_key & (pair_row == lax.rem(sel_m, rows)), 1.0, 0.0).astype(BF16)
    select_left = jnp.concatenate(
        [jnp.where(sel_key & (pair_row == i), 1.0, 0.0) for i in range(rows)], axis=0
    ).astype(BF16)
    wide_key = jnp.broadcast_to(lane_keys(amino), (amino, amino))
    key_col = jnp.sum(jnp.where(eye, wide_key, 0.0), axis=1, keepdims=True).astype(jnp.int32)
    key_col = jnp.concatenate([key_col] * rows, axis=0)
    slots = rows * padded
    col = iota((pairs, slots), 1)
    expand = jnp.where(
        (key_col == lax.rem(col, padded) + 1) & (iota((pairs, slots), 0) // amino == col // padded),
        1.0,
        0.0,
    ).astype(BF16)
    expand = jnp.concatenate([expand, expand], axis=1)
    if padded > live:
        outer_buf[live * inner :, :] = jnp.zeros(((padded - live) * inner, LANES), F32)

    for peer in same:
        slot = index_of(peer)
        arrived(right_all, slot, right_rsem)
        for k, other in enumerate(here):
            push(right_all.at[slot], right_all.at[slot], right_fsem.at[k, peer[1]], right_rsem.at[slot], other)
    for peer in everyone:
        arrived(left_all, index_of(peer), left_rsem)
        arrived(flag_all, index_of(peer), flag_rsem)
    for peer in here + far:
        arrived(right_all, index_of(peer), right_rsem)

    number = jnp.maximum(jnp.sum(flag_all[...], axis=0)[0:1, :], 1.0)
    left = left_all[...].reshape(n * seqs, LANES)
    right = right_all[...].reshape(n * seqs, live * inner)
    outer_buf[: live * inner, :] = lax.dot_general(
        right, left, (((0,), (0,)), ((), ())), preferred_element_type=F32
    )
    parts = [[] for _ in range(rows)]
    lane = iota((1, LANES), 1)
    for q in range(inner // reps):
        block = [outer_buf[pl.ds(q * reps + g, padded, stride=inner), :] for g in range(reps)]
        span = reps // 2
        while span:
            upper = (lane // (span * inner)) % 2 == 1
            new = list(block)
            for a in range(reps):
                if a & span:
                    continue
                b = a | span
                shift = span * inner
                new[a] = jnp.where(upper, pltpu.roll(block[b], shift, 1), block[a])
                new[b] = jnp.where(upper, block[b], pltpu.roll(block[a], LANES - shift, 1))
            block = new
            span //= 2
        for i in range(rows):
            parts[i].append(block[i])
    packed = jnp.concatenate([jnp.concatenate(p, axis=1) for p in parts], axis=0).astype(BF16)
    product = dot(packed, w_perm[...])
    high = product.astype(BF16)
    low = (product - high.astype(F32)).astype(BF16)
    projected = dot(expand, jnp.concatenate([high, low], axis=0))
    updated = base + projected / number
    pair = standardize(updated, cgain_ref[...]).astype(BF16)
    right_two = dot(pair, wedge_ref[:, 2 * width :])
    tri_right = (jax.nn.sigmoid(right_two[:, :width]) * right_two[:, width:]).astype(BF16)
    tri_all[me] = dot(select_right, tri_right).astype(BF16)
    for peer in near:
        push(tri_all.at[me], tri_all.at[me], tri_ssem.at[index_of(peer)], tri_rsem.at[me], peer)

    left_two = dot(pair, wedge_ref[:, : 2 * width])
    tri_left = (jax.nn.sigmoid(left_two[:, :width]) * left_two[:, width:]).astype(BF16)
    spread_left = dot(select_left, tri_left)
    gate = jax.nn.sigmoid(dot(pair, wgate_ref[...]))

    for peer in same:
        slot = index_of(peer)
        arrived(tri_all, slot, tri_rsem)
        for k, other in enumerate(here):
            push(tri_all.at[slot], tri_all.at[slot], tri_fsem.at[k, peer[1]], tri_rsem.at[slot], other)
    for peer in here + far:
        arrived(tri_all, index_of(peer), tri_rsem)

    pieces = SUB // rows
    sub = iota((SUB, LANES), 0)
    for d in range(0, n, pieces):
        blocks = [tri_all[d + h].astype(F32) for h in range(pieces)]
        for i in range(rows):
            mine = spread_left[i * sel_rows : (i + 1) * sel_rows]
            result = None
            for h in range(pieces):
                both = mine * blocks[h]
                acc = jnp.sum(both.reshape(sel_rows // SUB, SUB, LANES), axis=0)
                step = rows
                while step < SUB:
                    acc = acc + pltpu.roll(acc, step, 0)
                    step *= 2
                result = acc if result is None else jnp.where(sub // rows == h, acc, result)
            tri_buf[i * amino + d * rows : i * amino + d * rows + SUB, :] = result
    tri = standardize(tri_buf[...], tgain_ref[...]).astype(BF16)
    out_ref[...] = (updated + gate * dot(tri, wfin_ref[...])).astype(BF16)
    for copy in sends:
        copy.wait_send()


def on_device(nb, nz, x, hflags, aflags, classes, couple, hgain, wl, wr, wout, embed, cgain, wedge, wgate, wfin, tgain):
    n = nb * nz
    seqs, amino, depth = x.shape
    rows, _, width = couple.shape
    inner = wl.shape[1]
    live = amino - 3 * amino // 8
    padded = -(-live // SUB) * SUB
    dma = pltpu.SemaphoreType.DMA
    operands = (
        x.reshape(seqs * amino, depth), hflags.reshape(1, seqs), aflags.reshape(1, amino), classes,
        couple.reshape(rows * amino, width), hgain.reshape(1, depth), wl, wr, wout, embed,
        cgain.reshape(1, width), wedge, wgate, wfin, tgain.reshape(1, width),
    )
    out = pl.pallas_call(
        functools.partial(kernel, nb, nz),
        out_shape=jax.ShapeDtypeStruct((rows * amino, width), BF16),
        in_specs=[pl.BlockSpec(memory_space=pltpu.VMEM)] * len(operands),
        out_specs=pl.BlockSpec(memory_space=pltpu.VMEM),
        scratch_shapes=[
            pltpu.VMEM((n, SUB, LANES), F32),
            pltpu.VMEM((n, seqs, live * inner), BF16),
            pltpu.VMEM((n, seqs, LANES), BF16),
            pltpu.VMEM((n, seqs, LANES), BF16),
            pltpu.VMEM((n, live * rows, width), BF16),
            pltpu.VMEM((seqs * amino, LANES), F32),
            pltpu.VMEM((padded * inner, LANES), F32),
            pltpu.VMEM((inner * inner, width), F32),
            pltpu.VMEM((inner * inner, width), BF16),
            pltpu.VMEM((rows * amino, width), F32),
            dma((n,)), dma((n,)),
            dma((n,)), dma((n,)), dma((nb, nz)),
            dma((n,)), dma((n,)),
            dma((n,)), dma((n,)), dma((nb, nz)),
        ],
        compiler_params=pltpu.CompilerParams(collective_id=0, has_side_effects=True),
    )(*operands)
    return out.reshape(rows, amino, width)


def solution(mesh):
    split = ("rep", "branch", "dap")
    placed = (
        P(split, None, None), P(split), P("rep"), P(split, None), P(split, None, None),
        P(), P(), P(), P(), P(), P(), P(), P(), P(), P(),
    )
    return jax.shard_map(
        functools.partial(on_device, mesh.shape["branch"], mesh.shape["dap"]),
        mesh=mesh,
        in_specs=placed,
        out_specs=P(split, None, None),
        check_vma=False,
    )
```

```python
import functools

import jax
import jax.numpy as jnp
from jax import lax
from jax.experimental import pallas as pl
from jax.experimental.pallas import tpu as pltpu
from jax.sharding import PartitionSpec as P

F32 = jnp.float32
BF16 = jnp.bfloat16
MESH = pl.DeviceIdType.MESH
LANES = 128
SUB = 8


def iota(shape, axis):
    return lax.broadcasted_iota(jnp.int32, shape, axis)


def dot(a, b):
    return jnp.dot(a, b, preferred_element_type=F32)


def standardize(values, gain):
    mean = jnp.mean(values, axis=-1, keepdims=True)
    centred = values - mean
    spread = jnp.mean(centred * centred, axis=-1, keepdims=True)
    return centred * lax.rsqrt(spread + 1e-05) * gain


def kernel(
    nb, nz,
    x_ref, hflag_ref, aflag_ref, class_ref, couple_ref, hgain_ref, wl_ref, wr_ref, wout_ref,
    embed_ref, cgain_ref, wedge_ref, wgate_ref, wfin_ref, tgain_ref,
    out_ref,
    flag_all, right_all, left_send, left_all, tri_all, y_left, outer_buf, w_wide, w_perm, tri_buf,
    flag_ssem, flag_rsem, right_ssem, right_rsem, right_fsem, left_ssem, left_rsem,
    tri_ssem, tri_rsem, tri_fsem,
):
    n = nb * nz
    branch = lax.axis_index("branch")
    dap = lax.axis_index("dap")
    me = branch * nz + dap
    amino = aflag_ref.shape[1]
    seqs = hflag_ref.shape[1]
    rows = class_ref.shape[0]
    inner = wl_ref.shape[0]
    width = couple_ref.shape[1]
    reps = LANES // inner
    live = amino - 3 * amino // 8
    groups = live // reps
    pairs = rows * amino
    padded = -(-live // SUB) * SUB
    first = me * rows

    same = [(branch, lax.rem(dap + step, nz)) for step in range(1, nz)]
    here = [(lax.rem(branch + step, nb), dap) for step in range(1, nb)]
    far = [(b[0], z[1]) for b in here for z in same]
    near = same + here
    everyone = near + far

    def index_of(peer):
        return peer[0] * nz + peer[1]

    def target(peer):
        return {"branch": peer[0], "dap": peer[1]}

    barrier = pltpu.get_barrier_semaphore()
    for peer in everyone:
        pl.semaphore_signal(barrier, inc=1, device_id=target(peer), device_id_type=MESH)

    aflag = jnp.broadcast_to(aflag_ref[...].astype(F32), (SUB, amino)).astype(BF16)
    hflag32 = hflag_ref[...].astype(F32)
    hflag = jnp.broadcast_to(hflag32, (SUB, seqs)).astype(BF16)

    def lane_keys(lanes):
        r = iota((amino, lanes), 0)
        k = lax.rem(iota((amino, lanes), 1), amino)
        count = dot(aflag, (r <= k).astype(BF16))
        alive = dot(aflag, (r == k).astype(BF16))
        return (count * alive)[0:1, :]

    flag_all[me] = jnp.broadcast_to(jnp.sum(hflag32, axis=1, keepdims=True), (SUB, LANES))

    total = seqs * amino
    key_x = lane_keys(total)
    hlane = dot(hflag, (iota((seqs, total), 0) == iota((seqs, total), 1) // amino).astype(BF16))[0:1, :]
    key_x = jnp.where(hlane > 0.5, key_x, 0.0).astype(jnp.int32)
    m_row = iota((live * seqs, 1), 0)
    same_seq = lax.rem(m_row, seqs) == iota((1, total), 1) // amino
    gather_right = jnp.where((key_x == m_row // seqs + 1) & same_seq, 1.0, 0.0).astype(BF16)
    lane_group = iota((1, LANES), 1) // inner
    alane = dot(
        aflag,
        (iota((amino, amino * inner), 0) == iota((amino, amino * inner), 1) // inner).astype(BF16),
    )[0:1, :]

    normed = standardize(x_ref[...].astype(F32), hgain_ref[...]).astype(BF16)
    w_both = jnp.concatenate([wl_ref[...]] * reps + [wr_ref[...]] * reps, axis=0)
    sides = lax.dot_general(
        normed, w_both, (((1,), (1,)), ((), ())), preferred_element_type=F32
    )
    y_left[...] = sides[:, :LANES]
    right_rows = dot(gather_right, sides[:, LANES:].astype(BF16))
    for q in range(groups):
        block = right_rows[q * reps * seqs : (q * reps + 1) * seqs]
        for g in range(1, reps):
            start = (q * reps + g) * seqs
            block = jnp.where(lane_group == g, right_rows[start : start + seqs], block)
        right_all[me, :, q * LANES : (q + 1) * LANES] = block.astype(BF16)
    for d in range(n):
        block = y_left[pl.ds(d * rows, seqs, stride=amino), :]
        for g in range(1, rows):
            block = jnp.where(
                lane_group == g, y_left[pl.ds(d * rows + g, seqs, stride=amino), :], block
            )
        left_send[d] = (block * alane[:, d * LANES : (d + 1) * LANES]).astype(BF16)

    pl.semaphore_wait(barrier, n - 1)

    sends = []

    def push(src, dst, ssem, rsem, peer):
        copy = pltpu.make_async_remote_copy(
            src_ref=src, dst_ref=dst, send_sem=ssem, recv_sem=rsem,
            device_id=target(peer), device_id_type=MESH,
        )
        copy.start()
        sends.append(copy)

    def arrived(ref, slot, rsem):
        pltpu.make_async_remote_copy(
            src_ref=ref.at[slot], dst_ref=ref.at[slot], send_sem=rsem.at[slot],
            recv_sem=rsem.at[slot], device_id=target(everyone[0]), device_id_type=MESH,
        ).wait_recv()

    for peer in near:
        push(right_all.at[me], right_all.at[me], right_ssem.at[index_of(peer)], right_rsem.at[me], peer)
    for peer in everyone:
        d = index_of(peer)
        push(left_send.at[d], left_all.at[me], left_ssem.at[d], left_rsem.at[me], peer)
        push(flag_all.at[me], flag_all.at[me], flag_ssem.at[d], flag_rsem.at[me], peer)
    left_all[me] = left_send[me]

    w_wide[...] = wout_ref[...].astype(F32)
    for e in range(inner):
        w_perm[e * inner : (e + 1) * inner, :] = w_wide[
            pl.ds(e, inner, stride=inner), :
        ].astype(BF16)
    eye = iota((amino, amino), 0) == iota((amino, amino), 1)
    bins = embed_ref.shape[0]
    hot = []
    for i in range(rows):
        column = jnp.sum(
            jnp.where(eye, class_ref[i : i + 1, :], 0).astype(F32), axis=1, keepdims=True
        ).astype(jnp.int32)
        hot.append(jnp.where(column == iota((amino, bins), 1), 1.0, 0.0))
    onehot = jnp.concatenate(hot, axis=0).astype(BF16)
    base = couple_ref[...].astype(F32) + dot(onehot, embed_ref[...])

    key_pair = lane_keys(pairs)
    ilane = dot(
        aflag, (iota((amino, pairs), 0) == first + iota((amino, pairs), 1) // amino).astype(BF16)
    )[0:1, :]
    key_pair = jnp.where(ilane > 0.5, key_pair, 0.0).astype(jnp.int32)
    pair_row = iota((1, pairs), 1) // amino
    sel_rows = live * rows
    sel_m = iota((sel_rows, 1), 0)
    sel_key = key_pair == sel_m // rows + 1
    select_right = jnp.where(sel_key & (pair_row == lax.rem(sel_m, rows)), 1.0, 0.0).astype(BF16)
    select_left = jnp.concatenate(
        [jnp.where(sel_key & (pair_row == i), 1.0, 0.0) for i in range(rows)], axis=0
    ).astype(BF16)
    wide_key = jnp.broadcast_to(lane_keys(amino), (amino, amino))
    key_col = jnp.sum(jnp.where(eye, wide_key, 0.0), axis=1, keepdims=True).astype(jnp.int32)
    key_col = jnp.concatenate([key_col] * rows, axis=0)
    slots = rows * padded
    col = iota((pairs, slots), 1)
    expand = jnp.where(
        (key_col == lax.rem(col, padded) + 1) & (iota((pairs, slots), 0) // amino == col // padded),
        1.0,
        0.0,
    ).astype(BF16)
    expand = jnp.concatenate([expand, expand], axis=1)
    if padded > live:
        outer_buf[live * inner :, :] = jnp.zeros(((padded - live) * inner, LANES), F32)

    for peer in same:
        slot = index_of(peer)
        arrived(right_all, slot, right_rsem)
        for k, other in enumerate(here):
            push(right_all.at[slot], right_all.at[slot], right_fsem.at[k, peer[1]], right_rsem.at[slot], other)
    for peer in everyone:
        arrived(left_all, index_of(peer), left_rsem)
        arrived(flag_all, index_of(peer), flag_rsem)
    for peer in here + far:
        arrived(right_all, index_of(peer), right_rsem)

    number = jnp.maximum(jnp.sum(flag_all[...], axis=0)[0:1, :], 1.0)
    left = left_all[...].reshape(n * seqs, LANES)
    right = right_all[...].reshape(n * seqs, live * inner)
    outer_buf[: live * inner, :] = lax.dot_general(
        right, left, (((0,), (0,)), ((), ())), preferred_element_type=F32
    )
    parts = [[] for _ in range(rows)]
    lane = iota((1, LANES), 1)
    for q in range(inner // reps):
        block = [outer_buf[pl.ds(q * reps + g, padded, stride=inner), :] for g in range(reps)]
        span = reps // 2
        while span:
            upper = (lane // (span * inner)) % 2 == 1
            new = list(block)
            for a in range(reps):
                if a & span:
                    continue
                b = a | span
                shift = span * inner
                new[a] = jnp.where(upper, pltpu.roll(block[b], shift, 1), block[a])
                new[b] = jnp.where(upper, block[b], pltpu.roll(block[a], LANES - shift, 1))
            block = new
            span //= 2
        for i in range(rows):
            parts[i].append(block[i])
    packed = jnp.concatenate([jnp.concatenate(p, axis=1) for p in parts], axis=0).astype(BF16)
    product = dot(packed, w_perm[...])
    high = product.astype(BF16)
    low = (product - high.astype(F32)).astype(BF16)
    projected = dot(expand, jnp.concatenate([high, low], axis=0))
    updated = base + projected / number
    pair = standardize(updated, cgain_ref[...]).astype(BF16)
    right_two = dot(pair, wedge_ref[:, 2 * width :])
    tri_right = (jax.nn.sigmoid(right_two[:, :width]) * right_two[:, width:]).astype(BF16)
    tri_all[me] = dot(select_right, tri_right).astype(BF16)
    for peer in near:
        push(tri_all.at[me], tri_all.at[me], tri_ssem.at[index_of(peer)], tri_rsem.at[me], peer)

    left_two = dot(pair, wedge_ref[:, : 2 * width])
    tri_left = (jax.nn.sigmoid(left_two[:, :width]) * left_two[:, width:]).astype(BF16)
    spread_left = dot(select_left, tri_left)
    gate = jax.nn.sigmoid(dot(pair, wgate_ref[...]))

    for peer in same:
        slot = index_of(peer)
        arrived(tri_all, slot, tri_rsem)
        for k, other in enumerate(here):
            push(tri_all.at[slot], tri_all.at[slot], tri_fsem.at[k, peer[1]], tri_rsem.at[slot], other)
    for peer in here + far:
        arrived(tri_all, index_of(peer), tri_rsem)

    pieces = SUB // rows
    sub = iota((SUB, LANES), 0)
    for d in range(0, n, pieces):
        blocks = [tri_all[d + h].astype(F32) for h in range(pieces)]
        for i in range(rows):
            mine = spread_left[i * sel_rows : (i + 1) * sel_rows]
            result = None
            for h in range(pieces):
                both = mine * blocks[h]
                acc = jnp.sum(both.reshape(sel_rows // SUB, SUB, LANES), axis=0)
                step = rows
                while step < SUB:
                    acc = acc + pltpu.roll(acc, step, 0)
                    step *= 2
                result = acc if result is None else jnp.where(sub // rows == h, acc, result)
            tri_buf[i * amino + d * rows : i * amino + d * rows + SUB, :] = result
    tri = standardize(tri_buf[...], tgain_ref[...]).astype(BF16)
    out_ref[...] = (updated + gate * dot(tri, wfin_ref[...])).astype(BF16)
    for copy in sends:
        copy.wait_send()


def on_device(nb, nz, x, hflags, aflags, classes, couple, hgain, wl, wr, wout, embed, cgain, wedge, wgate, wfin, tgain):
    n = nb * nz
    seqs, amino, depth = x.shape
    rows, _, width = couple.shape
    inner = wl.shape[1]
    live = amino - 3 * amino // 8
    padded = -(-live // SUB) * SUB
    dma = pltpu.SemaphoreType.DMA
    operands = (
        x.reshape(seqs * amino, depth), hflags.reshape(1, seqs), aflags.reshape(1, amino), classes,
        couple.reshape(rows * amino, width), hgain.reshape(1, depth), wl.T, wr.T, wout, embed,
        cgain.reshape(1, width), wedge, wgate, wfin, tgain.reshape(1, width),
    )
    out = pl.pallas_call(
        functools.partial(kernel, nb, nz),
        out_shape=pltpu.VMEM((rows * amino, width), BF16),
        in_specs=[pl.BlockSpec(memory_space=pltpu.VMEM)] * len(operands),
        out_specs=pl.BlockSpec(memory_space=pltpu.VMEM),
        scratch_shapes=[
            pltpu.VMEM((n, SUB, LANES), F32),
            pltpu.VMEM((n, seqs, live * inner), BF16),
            pltpu.VMEM((n, seqs, LANES), BF16),
            pltpu.VMEM((n, seqs, LANES), BF16),
            pltpu.VMEM((n, live * rows, width), BF16),
            pltpu.VMEM((seqs * amino, LANES), F32),
            pltpu.VMEM((padded * inner, LANES), F32),
            pltpu.VMEM((inner * inner, width), F32),
            pltpu.VMEM((inner * inner, width), BF16),
            pltpu.VMEM((rows * amino, width), F32),
            dma((n,)), dma((n,)),
            dma((n,)), dma((n,)), dma((nb, nz)),
            dma((n,)), dma((n,)),
            dma((n,)), dma((n,)), dma((nb, nz)),
        ],
        compiler_params=pltpu.CompilerParams(collective_id=0, has_side_effects=True),
    )(*operands)
    return out.reshape(rows, amino, width)


def solution(mesh):
    split = ("rep", "branch", "dap")
    placed = (
        P(split, None, None), P(split), P("rep"), P(split, None), P(split, None, None),
        P(), P(), P(), P(), P(), P(), P(), P(), P(), P(),
    )
    return jax.shard_map(
        functools.partial(on_device, mesh.shape["branch"], mesh.shape["dap"]),
        mesh=mesh,
        in_specs=placed,
        out_specs=P(split, None, None),
        check_vma=False,
    )
```

```python
import functools

import jax
import jax.numpy as jnp
from jax import lax
from jax.experimental import pallas as pl
from jax.experimental.pallas import tpu as pltpu
from jax.sharding import PartitionSpec as P

F32 = jnp.float32
BF16 = jnp.bfloat16
MESH = pl.DeviceIdType.MESH
OPERANDS = 15
LANES = 128
SUB = 8


def iota(shape, axis):
    return lax.broadcasted_iota(jnp.int32, shape, axis)


def dot(a, b):
    return jnp.dot(a, b, preferred_element_type=F32)


def standardize(values, gain):
    mean = jnp.mean(values, axis=-1, keepdims=True)
    centred = values - mean
    spread = jnp.mean(centred * centred, axis=-1, keepdims=True)
    return centred * lax.rsqrt(spread + 1e-05) * gain


def kernel(
    nb, nz,
    *refs,
):
    operands, out_ref, held = refs[:OPERANDS], refs[OPERANDS], refs[OPERANDS + 1 : 2 * OPERANDS + 1]
    in_sem, *scratch = refs[2 * OPERANDS + 1 :]
    (x_ref, hflag_ref, aflag_ref, class_ref, couple_ref, hgain_ref, wl_ref, wr_ref, wout_ref,
     embed_ref, cgain_ref, wedge_ref, wgate_ref, wfin_ref, tgain_ref) = held
    (
    flag_all, right_all, left_send, left_all, tri_all, y_left, outer_buf, w_wide, w_perm, tri_buf,
    flag_ssem, flag_rsem, right_ssem, right_rsem, right_fsem, left_ssem, left_rsem,
    tri_ssem, tri_rsem, tri_fsem,
    ) = scratch
    n = nb * nz
    branch = lax.axis_index("branch")
    dap = lax.axis_index("dap")
    me = branch * nz + dap
    amino = aflag_ref.shape[1]
    seqs = hflag_ref.shape[1]
    rows = class_ref.shape[0]
    inner = wl_ref.shape[0]
    width = couple_ref.shape[1]
    reps = LANES // inner
    live = amino - 3 * amino // 8
    groups = live // reps
    pairs = rows * amino
    padded = -(-live // SUB) * SUB
    first = me * rows

    same = [(branch, lax.rem(dap + step, nz)) for step in range(1, nz)]
    here = [(lax.rem(branch + step, nb), dap) for step in range(1, nb)]
    far = [(b[0], z[1]) for b in here for z in same]
    near = same + here
    everyone = near + far

    def index_of(peer):
        return peer[0] * nz + peer[1]

    def target(peer):
        return {"branch": peer[0], "dap": peer[1]}

    barrier = pltpu.get_barrier_semaphore()
    for peer in everyone:
        pl.semaphore_signal(barrier, inc=1, device_id=target(peer), device_id_type=MESH)

    loads = {}
    for k in (2, 1, 0, 5, 6, 7, 8, 3, 4, 9, 10, 11, 12, 13, 14):
        loads[k] = pltpu.make_async_copy(operands[k], held[k], in_sem.at[k])
        loads[k].start()

    loads[2].wait()
    loads[1].wait()
    aflag = jnp.broadcast_to(aflag_ref[...].astype(F32), (SUB, amino)).astype(BF16)
    hflag32 = hflag_ref[...].astype(F32)
    hflag = jnp.broadcast_to(hflag32, (SUB, seqs)).astype(BF16)

    def lane_keys(lanes):
        r = iota((amino, lanes), 0)
        k = lax.rem(iota((amino, lanes), 1), amino)
        count = dot(aflag, (r <= k).astype(BF16))
        alive = dot(aflag, (r == k).astype(BF16))
        return (count * alive)[0:1, :]

    flag_all[me] = jnp.broadcast_to(jnp.sum(hflag32, axis=1, keepdims=True), (1, LANES))

    total = seqs * amino
    key_x = lane_keys(total)
    hlane = dot(hflag, (iota((seqs, total), 0) == iota((seqs, total), 1) // amino).astype(BF16))[0:1, :]
    key_x = jnp.where(hlane > 0.5, key_x, 0.0).astype(jnp.int32)
    m_row = iota((live * seqs, 1), 0)
    same_seq = lax.rem(m_row, seqs) == iota((1, total), 1) // amino
    gather_right = jnp.where((key_x == m_row // seqs + 1) & same_seq, 1.0, 0.0).astype(BF16)
    lane_group = iota((1, LANES), 1) // inner
    alane = dot(
        aflag,
        (iota((amino, amino * inner), 0) == iota((amino, amino * inner), 1) // inner).astype(BF16),
    )[0:1, :]

    for k in (0, 5, 6, 7):
        loads[k].wait()
    normed = standardize(x_ref[...].astype(F32), hgain_ref[...]).astype(BF16)
    w_both = jnp.concatenate([wl_ref[...]] * reps + [wr_ref[...]] * reps, axis=0)
    sides = lax.dot_general(
        normed, w_both, (((1,), (1,)), ((), ())), preferred_element_type=F32
    )
    y_left[...] = sides[:, :LANES]
    right_rows = dot(gather_right, sides[:, LANES:].astype(BF16))
    for q in range(groups):
        block = right_rows[q * reps * seqs : (q * reps + 1) * seqs]
        for g in range(1, reps):
            start = (q * reps + g) * seqs
            block = jnp.where(lane_group == g, right_rows[start : start + seqs], block)
        right_all[me, :, q * LANES : (q + 1) * LANES] = block.astype(BF16)
    for d in range(n):
        block = y_left[pl.ds(d * rows, seqs, stride=amino), :]
        for g in range(1, rows):
            block = jnp.where(
                lane_group == g, y_left[pl.ds(d * rows + g, seqs, stride=amino), :], block
            )
        left_send[d] = (block * alane[:, d * LANES : (d + 1) * LANES]).astype(BF16)

    pl.semaphore_wait(barrier, n - 1)

    sends = []

    def push(src, dst, ssem, rsem, peer):
        copy = pltpu.make_async_remote_copy(
            src_ref=src, dst_ref=dst, send_sem=ssem, recv_sem=rsem,
            device_id=target(peer), device_id_type=MESH,
        )
        copy.start()
        sends.append(copy)

    def arrived(ref, slot, rsem):
        pltpu.make_async_remote_copy(
            src_ref=ref.at[slot], dst_ref=ref.at[slot], send_sem=rsem.at[slot],
            recv_sem=rsem.at[slot], device_id=target(everyone[0]), device_id_type=MESH,
        ).wait_recv()

    for peer in everyone:
        d = index_of(peer)
        push(flag_all.at[me], flag_all.at[me], flag_ssem.at[d], flag_rsem.at[me], peer)
    for peer in near:
        push(right_all.at[me], right_all.at[me], right_ssem.at[index_of(peer)], right_rsem.at[me], peer)
    for peer in everyone:
        d = index_of(peer)
        push(left_send.at[d], left_all.at[me], left_ssem.at[d], left_rsem.at[me], peer)
    left_all[me] = left_send[me]

    for k in (8, 3, 4, 9, 10, 11, 12, 13, 14):
        loads[k].wait()
    w_wide[...] = wout_ref[...].astype(F32)
    for e in range(inner):
        w_perm[e * inner : (e + 1) * inner, :] = w_wide[
            pl.ds(e, inner, stride=inner), :
        ].astype(BF16)
    eye = iota((amino, amino), 0) == iota((amino, amino), 1)
    bins = embed_ref.shape[0]
    hot = []
    for i in range(rows):
        column = jnp.sum(
            jnp.where(eye, class_ref[i : i + 1, :], 0).astype(F32), axis=1, keepdims=True
        ).astype(jnp.int32)
        hot.append(jnp.where(column == iota((amino, bins), 1), 1.0, 0.0))
    onehot = jnp.concatenate(hot, axis=0).astype(BF16)
    base = couple_ref[...].astype(F32) + dot(onehot, embed_ref[...])

    key_pair = lane_keys(pairs)
    ilane = dot(
        aflag, (iota((amino, pairs), 0) == first + iota((amino, pairs), 1) // amino).astype(BF16)
    )[0:1, :]
    key_pair = jnp.where(ilane > 0.5, key_pair, 0.0).astype(jnp.int32)
    pair_row = iota((1, pairs), 1) // amino
    sel_rows = live * rows
    sel_m = iota((sel_rows, 1), 0)
    sel_key = key_pair == sel_m // rows + 1
    select_right = jnp.where(sel_key & (pair_row == lax.rem(sel_m, rows)), 1.0, 0.0).astype(BF16)
    select_left = jnp.concatenate(
        [jnp.where(sel_key & (pair_row == i), 1.0, 0.0) for i in range(rows)], axis=0
    ).astype(BF16)
    wide_key = jnp.broadcast_to(lane_keys(amino), (amino, amino))
    key_col = jnp.sum(jnp.where(eye, wide_key, 0.0), axis=1, keepdims=True).astype(jnp.int32)
    key_col = jnp.concatenate([key_col] * rows, axis=0)
    slots = rows * padded
    col = iota((pairs, slots), 1)
    expand = jnp.where(
        (key_col == lax.rem(col, padded) + 1) & (iota((pairs, slots), 0) // amino == col // padded),
        1.0,
        0.0,
    ).astype(BF16)
    expand = jnp.concatenate([expand, expand], axis=1)
    if padded > live:
        outer_buf[live * inner :, :] = jnp.zeros(((padded - live) * inner, LANES), F32)

    for peer in same:
        slot = index_of(peer)
        arrived(right_all, slot, right_rsem)
        for k, other in enumerate(here):
            push(right_all.at[slot], right_all.at[slot], right_fsem.at[k, peer[1]], right_rsem.at[slot], other)
    for peer in everyone:
        arrived(left_all, index_of(peer), left_rsem)
        arrived(flag_all, index_of(peer), flag_rsem)
    for peer in here + far:
        arrived(right_all, index_of(peer), right_rsem)

    number = jnp.maximum(jnp.sum(flag_all[...], axis=0), 1.0)
    left = left_all[...].reshape(n * seqs, LANES)
    right = right_all[...].reshape(n * seqs, live * inner)
    outer_buf[: live * inner, :] = lax.dot_general(
        right, left, (((0,), (0,)), ((), ())), preferred_element_type=F32
    )
    parts = [[] for _ in range(rows)]
    lane = iota((1, LANES), 1)
    for q in range(inner // reps):
        block = [outer_buf[pl.ds(q * reps + g, padded, stride=inner), :] for g in range(reps)]
        span = reps // 2
        while span:
            upper = (lane // (span * inner)) % 2 == 1
            new = list(block)
            for a in range(reps):
                if a & span:
                    continue
                b = a | span
                shift = span * inner
                new[a] = jnp.where(upper, pltpu.roll(block[b], shift, 1), block[a])
                new[b] = jnp.where(upper, block[b], pltpu.roll(block[a], LANES - shift, 1))
            block = new
            span //= 2
        for i in range(rows):
            parts[i].append(block[i])
    packed = jnp.concatenate([jnp.concatenate(p, axis=1) for p in parts], axis=0).astype(BF16)
    product = dot(packed, w_perm[...])
    high = product.astype(BF16)
    low = (product - high.astype(F32)).astype(BF16)
    projected = dot(expand, jnp.concatenate([high, low], axis=0))
    updated = base + projected / number
    pair = standardize(updated, cgain_ref[...]).astype(BF16)
    right_two = dot(pair, wedge_ref[:, 2 * width :])
    tri_right = (jax.nn.sigmoid(right_two[:, :width]) * right_two[:, width:]).astype(BF16)
    tri_all[me] = dot(select_right, tri_right).astype(BF16)
    for peer in near:
        push(tri_all.at[me], tri_all.at[me], tri_ssem.at[index_of(peer)], tri_rsem.at[me], peer)

    left_two = dot(pair, wedge_ref[:, : 2 * width])
    tri_left = (jax.nn.sigmoid(left_two[:, :width]) * left_two[:, width:]).astype(BF16)
    spread_left = dot(select_left, tri_left)
    gate = jax.nn.sigmoid(dot(pair, wgate_ref[...]))

    for peer in same:
        slot = index_of(peer)
        arrived(tri_all, slot, tri_rsem)
        for k, other in enumerate(here):
            push(tri_all.at[slot], tri_all.at[slot], tri_fsem.at[k, peer[1]], tri_rsem.at[slot], other)
    for peer in here + far:
        arrived(tri_all, index_of(peer), tri_rsem)

    pieces = SUB // rows
    sub = iota((SUB, LANES), 0)
    for d in range(0, n, pieces):
        blocks = [tri_all[d + h].astype(F32) for h in range(pieces)]
        for i in range(rows):
            mine = spread_left[i * sel_rows : (i + 1) * sel_rows]
            result = None
            for h in range(pieces):
                both = mine * blocks[h]
                acc = jnp.sum(both.reshape(sel_rows // SUB, SUB, LANES), axis=0)
                step = rows
                while step < SUB:
                    acc = acc + pltpu.roll(acc, step, 0)
                    step *= 2
                result = acc if result is None else jnp.where(sub // rows == h, acc, result)
            tri_buf[i * amino + d * rows : i * amino + d * rows + SUB, :] = result
    tri = standardize(tri_buf[...], tgain_ref[...]).astype(BF16)
    out_ref[...] = (updated + gate * dot(tri, wfin_ref[...])).astype(BF16)
    for copy in sends:
        copy.wait_send()


def on_device(nb, nz, x, hflags, aflags, classes, couple, hgain, wl, wr, wout, embed, cgain, wedge, wgate, wfin, tgain):
    n = nb * nz
    seqs, amino, depth = x.shape
    rows, _, width = couple.shape
    inner = wl.shape[1]
    live = amino - 3 * amino // 8
    padded = -(-live // SUB) * SUB
    dma = pltpu.SemaphoreType.DMA
    operands = (
        x.reshape(seqs * amino, depth), hflags.reshape(1, seqs), aflags.reshape(1, amino), classes,
        couple.reshape(rows * amino, width), hgain.reshape(1, depth), wl.T, wr.T, wout, embed,
        cgain.reshape(1, width), wedge, wgate, wfin, tgain.reshape(1, width),
    )
    out = pl.pallas_call(
        functools.partial(kernel, nb, nz),
        out_shape=pltpu.VMEM((rows * amino, width), BF16),
        in_specs=[pl.BlockSpec(memory_space=pl.ANY)] * OPERANDS,
        out_specs=pl.BlockSpec(memory_space=pltpu.VMEM),
        scratch_shapes=[pltpu.VMEM(a.shape, a.dtype) for a in operands]
        + [
            dma((OPERANDS,)),
            pltpu.VMEM((n, 1, LANES), F32),
            pltpu.VMEM((n, seqs, live * inner), BF16),
            pltpu.VMEM((n, seqs, LANES), BF16),
            pltpu.VMEM((n, seqs, LANES), BF16),
            pltpu.VMEM((n, live * rows, width), BF16),
            pltpu.VMEM((seqs * amino, LANES), F32),
            pltpu.VMEM((padded * inner, LANES), F32),
            pltpu.VMEM((inner * inner, width), F32),
            pltpu.VMEM((inner * inner, width), BF16),
            pltpu.VMEM((rows * amino, width), F32),
            dma((n,)), dma((n,)),
            dma((n,)), dma((n,)), dma((nb, nz)),
            dma((n,)), dma((n,)),
            dma((n,)), dma((n,)), dma((nb, nz)),
        ],
        compiler_params=pltpu.CompilerParams(collective_id=0, has_side_effects=True),
    )(*operands)
    return out.reshape(rows, amino, width)


def solution(mesh):
    split = ("rep", "branch", "dap")
    placed = (
        P(split, None, None), P(split), P("rep"), P(split, None), P(split, None, None),
        P(), P(), P(), P(), P(), P(), P(), P(), P(), P(),
    )
    return jax.shard_map(
        functools.partial(on_device, mesh.shape["branch"], mesh.shape["dap"]),
        mesh=mesh,
        in_specs=placed,
        out_specs=P(split, None, None),
        check_vma=False,
    )
```

```python
import functools

import jax
import jax.numpy as jnp
from jax import lax
from jax.experimental import pallas as pl
from jax.experimental.pallas import tpu as pltpu
from jax.sharding import PartitionSpec as P

F32 = jnp.float32
BF16 = jnp.bfloat16
MESH = pl.DeviceIdType.MESH
OPERANDS = 15
LANES = 128
SUB = 8


def iota(shape, axis):
    return lax.broadcasted_iota(jnp.int32, shape, axis)


def dot(a, b):
    return jnp.dot(a, b, preferred_element_type=F32)


def standardize(values, gain):
    mean = jnp.mean(values, axis=-1, keepdims=True)
    centred = values - mean
    spread = jnp.mean(centred * centred, axis=-1, keepdims=True)
    return centred * lax.rsqrt(spread + 1e-05) * gain


def kernel(
    nb, nz,
    *refs,
):
    operands, out_ref, held = refs[:OPERANDS], refs[OPERANDS], refs[OPERANDS + 1 : 2 * OPERANDS + 1]
    in_sem, *scratch = refs[2 * OPERANDS + 1 :]
    (x_ref, hflag_ref, aflag_ref, class_ref, couple_ref, hgain_ref, wl_ref, wr_ref, wout_ref,
     embed_ref, cgain_ref, wedge_ref, wgate_ref, wfin_ref, tgain_ref) = held
    (
    flag_all, right_all, left_send, left_all, tri_all, y_left, outer_buf, w_wide, w_perm, tri_buf,
    flag_ssem, flag_rsem, right_ssem, right_rsem, right_fsem, left_ssem, left_rsem,
    tri_ssem, tri_rsem, tri_fsem,
    ) = scratch
    n = nb * nz
    branch = lax.axis_index("branch")
    dap = lax.axis_index("dap")
    me = branch * nz + dap
    amino = aflag_ref.shape[1]
    seqs = hflag_ref.shape[1]
    rows = class_ref.shape[0]
    inner = wl_ref.shape[0]
    width = couple_ref.shape[1]
    reps = LANES // inner
    live = amino - 3 * amino // 8
    groups = live // reps
    pairs = rows * amino
    padded = -(-live // SUB) * SUB
    first = me * rows

    same = [(branch, lax.rem(dap + step, nz)) for step in range(1, nz)]
    here = [(lax.rem(branch + step, nb), dap) for step in range(1, nb)]
    far = [(b[0], z[1]) for b in here for z in same]
    near = same + here
    everyone = near + far

    def index_of(peer):
        return peer[0] * nz + peer[1]

    def target(peer):
        return {"branch": peer[0], "dap": peer[1]}

    barrier = pltpu.get_barrier_semaphore()
    for peer in everyone:
        pl.semaphore_signal(barrier, inc=1, device_id=target(peer), device_id_type=MESH)

    loads = {}
    for k in (2, 1, 0, 5, 6, 7, 8, 3, 4, 9, 10, 11, 12, 13, 14):
        loads[k] = pltpu.make_async_copy(operands[k], held[k], in_sem.at[k])
        loads[k].start()

    loads[2].wait()
    loads[1].wait()
    aflag = jnp.broadcast_to(aflag_ref[...].astype(F32), (SUB, amino)).astype(BF16)
    hflag32 = hflag_ref[...].astype(F32)
    hflag = jnp.broadcast_to(hflag32, (SUB, seqs)).astype(BF16)

    def lane_keys(lanes):
        r = iota((amino, lanes), 0)
        k = lax.rem(iota((amino, lanes), 1), amino)
        count = dot(aflag, (r <= k).astype(BF16))
        alive = dot(aflag, (r == k).astype(BF16))
        return (count * alive)[0:1, :]

    flag_all[me] = jnp.broadcast_to(jnp.sum(hflag32, axis=1, keepdims=True), (1, LANES))

    total = seqs * amino
    key_x = lane_keys(total)
    hlane = dot(hflag, (iota((seqs, total), 0) == iota((seqs, total), 1) // amino).astype(BF16))[0:1, :]
    key_x = jnp.where(hlane > 0.5, key_x, 0.0).astype(jnp.int32)
    m_row = iota((live * seqs, 1), 0)
    same_seq = lax.rem(m_row, seqs) == iota((1, total), 1) // amino
    gather_right = jnp.where((key_x == m_row // seqs + 1) & same_seq, 1.0, 0.0).astype(BF16)
    lane_group = iota((1, LANES), 1) // inner
    alane = dot(
        aflag,
        (iota((amino, amino * inner), 0) == iota((amino, amino * inner), 1) // inner).astype(BF16),
    )[0:1, :]

    for k in (0, 5, 6, 7):
        loads[k].wait()
    normed = standardize(x_ref[...].astype(F32), hgain_ref[...]).astype(BF16)
    w_both = jnp.concatenate([wl_ref[...]] * reps + [wr_ref[...]] * reps, axis=0)
    sides = lax.dot_general(
        normed, w_both, (((1,), (1,)), ((), ())), preferred_element_type=F32
    )
    y_left[...] = sides[:, :LANES]
    right_rows = dot(gather_right, sides[:, LANES:].astype(BF16))
    for q in range(groups):
        block = right_rows[q * reps * seqs : (q * reps + 1) * seqs]
        for g in range(1, reps):
            start = (q * reps + g) * seqs
            block = jnp.where(lane_group == g, right_rows[start : start + seqs], block)
        right_all[me, :, q * LANES : (q + 1) * LANES] = block.astype(BF16)
    for d in range(n):
        block = y_left[pl.ds(d * rows, seqs, stride=amino), :]
        for g in range(1, rows):
            block = jnp.where(
                lane_group == g, y_left[pl.ds(d * rows + g, seqs, stride=amino), :], block
            )
        left_send[d] = (block * alane[:, d * LANES : (d + 1) * LANES]).astype(BF16)

    pl.semaphore_wait(barrier, n - 1)

    sends = []

    def push(src, dst, ssem, rsem, peer):
        copy = pltpu.make_async_remote_copy(
            src_ref=src, dst_ref=dst, send_sem=ssem, recv_sem=rsem,
            device_id=target(peer), device_id_type=MESH,
        )
        copy.start()
        sends.append(copy)

    def arrived(ref, slot, rsem):
        pltpu.make_async_remote_copy(
            src_ref=ref.at[slot], dst_ref=ref.at[slot], send_sem=rsem.at[slot],
            recv_sem=rsem.at[slot], device_id=target(everyone[0]), device_id_type=MESH,
        ).wait_recv()

    for peer in everyone:
        d = index_of(peer)
        push(flag_all.at[me], flag_all.at[me], flag_ssem.at[d], flag_rsem.at[me], peer)
    for peer in near:
        push(right_all.at[me], right_all.at[me], right_ssem.at[index_of(peer)], right_rsem.at[me], peer)
    for peer in everyone:
        d = index_of(peer)
        push(left_send.at[d], left_all.at[me], left_ssem.at[d], left_rsem.at[me], peer)
    left_all[me] = left_send[me]

    for k in (8, 3, 4, 9, 10, 11, 12, 13, 14):
        loads[k].wait()
    w_wide[...] = wout_ref[...].astype(F32)
    for e in range(inner):
        w_perm[e * inner : (e + 1) * inner, :] = w_wide[
            pl.ds(e, inner, stride=inner), :
        ].astype(BF16)
    eye = iota((amino, amino), 0) == iota((amino, amino), 1)
    bins = embed_ref.shape[0]
    hot = []
    for i in range(rows):
        column = jnp.sum(
            jnp.where(eye, class_ref[i : i + 1, :], 0).astype(F32), axis=1, keepdims=True
        ).astype(jnp.int32)
        hot.append(jnp.where(column == iota((amino, bins), 1), 1.0, 0.0))
    onehot = jnp.concatenate(hot, axis=0).astype(BF16)
    base = couple_ref[...].astype(F32) + dot(onehot, embed_ref[...])

    key_pair = lane_keys(pairs)
    ilane = dot(
        aflag, (iota((amino, pairs), 0) == first + iota((amino, pairs), 1) // amino).astype(BF16)
    )[0:1, :]
    key_pair = jnp.where(ilane > 0.5, key_pair, 0.0).astype(jnp.int32)
    pair_row = iota((1, pairs), 1) // amino
    sel_rows = live * rows
    sel_m = iota((sel_rows, 1), 0)
    sel_key = key_pair == sel_m // rows + 1
    select_right = jnp.where(sel_key & (pair_row == lax.rem(sel_m, rows)), 1.0, 0.0).astype(BF16)
    select_left = jnp.concatenate(
        [jnp.where(sel_key & (pair_row == i), 1.0, 0.0) for i in range(rows)], axis=0
    ).astype(BF16)
    wide_key = jnp.broadcast_to(lane_keys(amino), (amino, amino))
    key_col = jnp.sum(jnp.where(eye, wide_key, 0.0), axis=1, keepdims=True).astype(jnp.int32)
    key_col = jnp.concatenate([key_col] * rows, axis=0)
    slots = rows * padded
    col = iota((pairs, slots), 1)
    expand = jnp.where(
        (key_col == lax.rem(col, padded) + 1) & (iota((pairs, slots), 0) // amino == col // padded),
        1.0,
        0.0,
    ).astype(BF16)
    expand = jnp.concatenate([expand, expand], axis=1)
    if padded > live:
        outer_buf[live * inner :, :] = jnp.zeros(((padded - live) * inner, LANES), F32)

    for peer in same:
        slot = index_of(peer)
        arrived(right_all, slot, right_rsem)
        for k, other in enumerate(here):
            push(right_all.at[slot], right_all.at[slot], right_fsem.at[k, peer[1]], right_rsem.at[slot], other)
    for peer in everyone:
        arrived(left_all, index_of(peer), left_rsem)
        arrived(flag_all, index_of(peer), flag_rsem)
    for peer in here + far:
        arrived(right_all, index_of(peer), right_rsem)

    number = jnp.maximum(jnp.sum(flag_all[...], axis=0), 1.0)
    left = left_all[...].reshape(n * seqs, LANES)
    right = right_all[...].reshape(n * seqs, live * inner)
    outer_buf[: live * inner, :] = lax.dot_general(
        right, left, (((0,), (0,)), ((), ())), preferred_element_type=F32
    )
    parts = [[] for _ in range(rows)]
    lane = iota((1, LANES), 1)
    for q in range(inner // reps):
        block = [outer_buf[pl.ds(q * reps + g, padded, stride=inner), :] for g in range(reps)]
        span = reps // 2
        while span:
            upper = (lane // (span * inner)) % 2 == 1
            new = list(block)
            for a in range(reps):
                if a & span:
                    continue
                b = a | span
                shift = span * inner
                new[a] = jnp.where(upper, pltpu.roll(block[b], shift, 1), block[a])
                new[b] = jnp.where(upper, block[b], pltpu.roll(block[a], LANES - shift, 1))
            block = new
            span //= 2
        for i in range(rows):
            parts[i].append(block[i])
    packed = jnp.concatenate([jnp.concatenate(p, axis=1) for p in parts], axis=0).astype(BF16)
    product = dot(packed, w_perm[...])
    high = product.astype(BF16)
    low = (product - high.astype(F32)).astype(BF16)
    projected = dot(expand, jnp.concatenate([high, low], axis=0))
    updated = base + projected / number
    pair = standardize(updated, cgain_ref[...]).astype(BF16)
    right_two = dot(pair, wedge_ref[:, 2 * width :])
    tri_right = (jax.nn.sigmoid(right_two[:, :width]) * right_two[:, width:]).astype(BF16)
    tri_all[me] = dot(select_right, tri_right).astype(BF16)
    for peer in near:
        push(tri_all.at[me], tri_all.at[me], tri_ssem.at[index_of(peer)], tri_rsem.at[me], peer)

    left_two = dot(pair, wedge_ref[:, : 2 * width])
    tri_left = (jax.nn.sigmoid(left_two[:, :width]) * left_two[:, width:]).astype(BF16)
    spread_left = dot(select_left, tri_left)
    gate = jax.nn.sigmoid(dot(pair, wgate_ref[...]))

    def passing(peer):
        slot = index_of(peer)
        arrived(tri_all, slot, tri_rsem)
        for k, other in enumerate(here):
            push(tri_all.at[slot], tri_all.at[slot], tri_fsem.at[k, peer[1]], tri_rsem.at[slot], other)

    pieces = SUB // rows
    sub = iota((SUB, LANES), 0)

    def triangle(start):
        blocks = [tri_all[start + h].astype(F32) for h in range(pieces)]
        for i in range(rows):
            mine = spread_left[i * sel_rows : (i + 1) * sel_rows]
            result = None
            for h in range(pieces):
                both = mine * blocks[h]
                acc = jnp.sum(both.reshape(sel_rows // SUB, SUB, LANES), axis=0)
                step = rows
                while step < SUB:
                    acc = acc + pltpu.roll(acc, step, 0)
                    step *= 2
                result = acc if result is None else jnp.where(sub // rows == h, acc, result)
            row = i * amino + start * rows
            tri_buf[pl.ds(row if isinstance(row, int) else pl.multiple_of(row, SUB), SUB), :] = result

    for peer in same:
        passing(peer)
    if nz % pieces == 0:
        for b in [branch] + [o[0] for o in here]:
            if b is not branch:
                for peer in here + far:
                    if peer[0] is b:
                        arrived(tri_all, index_of(peer), tri_rsem)
            for z in range(0, nz, pieces):
                triangle(b * nz + z)
    else:
        for peer in here + far:
            arrived(tri_all, index_of(peer), tri_rsem)
        for d in range(0, n, pieces):
            triangle(d)
    tri = standardize(tri_buf[...], tgain_ref[...]).astype(BF16)
    out_ref[...] = (updated + gate * dot(tri, wfin_ref[...])).astype(BF16)
    for copy in sends:
        copy.wait_send()


def on_device(nb, nz, x, hflags, aflags, classes, couple, hgain, wl, wr, wout, embed, cgain, wedge, wgate, wfin, tgain):
    n = nb * nz
    seqs, amino, depth = x.shape
    rows, _, width = couple.shape
    inner = wl.shape[1]
    live = amino - 3 * amino // 8
    padded = -(-live // SUB) * SUB
    dma = pltpu.SemaphoreType.DMA
    operands = (
        x.reshape(seqs * amino, depth), hflags.reshape(1, seqs), aflags.reshape(1, amino), classes,
        couple.reshape(rows * amino, width), hgain.reshape(1, depth), wl.T, wr.T, wout, embed,
        cgain.reshape(1, width), wedge, wgate, wfin, tgain.reshape(1, width),
    )
    out = pl.pallas_call(
        functools.partial(kernel, nb, nz),
        out_shape=pltpu.VMEM((rows * amino, width), BF16),
        in_specs=[pl.BlockSpec(memory_space=pl.ANY)] * OPERANDS,
        out_specs=pl.BlockSpec(memory_space=pltpu.VMEM),
        scratch_shapes=[pltpu.VMEM(a.shape, a.dtype) for a in operands]
        + [
            dma((OPERANDS,)),
            pltpu.VMEM((n, 1, LANES), F32),
            pltpu.VMEM((n, seqs, live * inner), BF16),
            pltpu.VMEM((n, seqs, LANES), BF16),
            pltpu.VMEM((n, seqs, LANES), BF16),
            pltpu.VMEM((n, live * rows, width), BF16),
            pltpu.VMEM((seqs * amino, LANES), F32),
            pltpu.VMEM((padded * inner, LANES), F32),
            pltpu.VMEM((inner * inner, width), F32),
            pltpu.VMEM((inner * inner, width), BF16),
            pltpu.VMEM((rows * amino, width), F32),
            dma((n,)), dma((n,)),
            dma((n,)), dma((n,)), dma((nb, nz)),
            dma((n,)), dma((n,)),
            dma((n,)), dma((n,)), dma((nb, nz)),
        ],
        compiler_params=pltpu.CompilerParams(collective_id=0, has_side_effects=True),
    )(*operands)
    return out.reshape(rows, amino, width)


def solution(mesh):
    split = ("rep", "branch", "dap")
    placed = (
        P(split, None, None), P(split), P("rep"), P(split, None), P(split, None, None),
        P(), P(), P(), P(), P(), P(), P(), P(), P(), P(),
    )
    return jax.shard_map(
        functools.partial(on_device, mesh.shape["branch"], mesh.shape["dap"]),
        mesh=mesh,
        in_specs=placed,
        out_specs=P(split, None, None),
        check_vma=False,
    )
```
